32 devices in a mesh: sector: 4 (over x, core), op: 8 (over z, y).
Axes of the slice: x: 2, y: 2, z: 4, core: 2. Of those that a mesh axis runs over, the one named last changes fastest.
Arguments:
- wave: float32 [8, 768, 768], P('sector', 'op'), may hold values from -6 to 6
- onsite: float32 [8, 768, 768], P('sector', 'op'), may hold values from -2 to 2
- left_ops: float32 [8, 16, 768, 768], P('sector', 'op'), may hold values from -0.21875 to 0.21875
- right_ops: float32 [8, 16, 768, 768], P('sector', 'op'), may hold values from -0.0546875 to 0.0546875
- coupling: int32 [8, 16], P('sector', 'op'), may hold values from 0 to 2
Outputs:
- sigma: float32 [8, 768, 768], P('sector', 'op')
- correction: float32 [8, 768, 768], P('sector', 'op')
The draws below stay inside these ranges and needn't reach their ends.
All inputs are finite; a program needn't handle non-finite values.
Results may differ from the reference program's by a relative error of at most 0.0001.
Values sent between devices are 32-bit elements; how exact they have to be, the bound alone decides.
No kernel may reach another device: no remote copies, remote signals or barrier semaphores. Data moves between devices by JAX's collectives and lax.ppermute only.
A program may use at most 128 MiB of HBM per device.

```python
import jax
import jax.numpy as jnp
from jax import lax

M = 768
SECTORS = 8
PAIRS = 16


def set_ends(result, stream_key, least, top_value):
    place = [jax.random.randint(jax.random.fold_in(stream_key, axis), (), 0, length) for axis, length in enumerate(result.shape)]
    longest = result.shape.index(max(result.shape))
    next_to = place[:longest] + [(place[longest] + 1) % result.shape[longest]] + place[longest + 1:]
    return result.at[tuple(place)].set(least).at[tuple(next_to)].set(top_value)


def level_of(key, dims, cuts, low, top_value):
    loudness = 1.0
    for position, parts in cuts:
        draws = jax.random.uniform(jax.random.fold_in(jax.random.fold_in(key, 6), position), (parts,), jnp.float32, low / len(cuts), top_value / len(cuts))
        loudness = loudness * jnp.repeat(jnp.exp(draws), dims[position] // parts).reshape((-1,) + (1,) * (len(dims) - 1 - position))
    return loudness


def gaussian(own_key, shape, width, limit, shards=(), dtype=jnp.bfloat16):
    array = jax.random.normal(own_key, shape, jnp.float32) * width
    if len(shards) > 0:
        array = level_of(own_key, shape, shards, -0.22, 0.18) * array
    return jnp.clip(array, min=-limit, max=limit).astype(dtype)


def setup_inputs(seed: int = 0) -> dict:
    key_of = jax.random.split(jax.random.key(seed), 6)
    return {
        "wave": gaussian(key_of[0], (SECTORS, M, M), 1.0, 6.0, ((0, 4), (1, 8)), jnp.float32),
        "onsite": jnp.clip(jax.random.uniform(key_of[1], (SECTORS, M, M), jnp.float32, -2.0, 2.0) * level_of(key_of[1], (SECTORS, M, M), ((0, 4), (1, 8)), -0.4, 0.0), -2.0, 2.0),
        "left_ops": gaussian(key_of[2], (SECTORS, PAIRS, M, M), M ** -0.5, 0.21875, ((0, 4), (1, 8)), jnp.float32),
        "right_ops": gaussian(key_of[3], (SECTORS, PAIRS, M, M), (M * PAIRS) ** -0.5, 0.0546875, ((0, 4), (1, 8)), jnp.float32),
        "coupling": set_ends(jax.random.randint(key_of[4], (SECTORS, PAIRS), 0, 3), jax.random.fold_in(key_of[4], 1), 0, 2).astype(jnp.int32),
    }


def reference(wave, onsite, left_ops, right_ops, coupling):
    highest = lax.Precision.HIGHEST
    weights = coupling.astype(jnp.float32)
    following = jnp.roll(wave, -1, axis=0)

    def sector_terms(items):
        lefts, rights, weight, own, ahead = items

        def pair_step(acc, item):
            left, right, scale = item
            fwd = jnp.dot(jnp.dot(left, own, precision=highest), right.T, precision=highest)
            back = jnp.dot(jnp.dot(left.T, ahead, precision=highest), right, precision=highest)
            return ((acc[0] + scale * fwd, acc[1] + scale * back), None)
        zero = jnp.zeros_like(own)
        (fwd, back), _ = lax.scan(pair_step, (zero, zero), (lefts, rights, weight))
        return (fwd, back)
    forward, backward = lax.map(sector_terms, (left_ops, right_ops, weights, wave, following))
    sigma = onsite * wave + backward + jnp.roll(forward, 1, axis=0)
    total = wave.shape[0] * wave.shape[1] * wave.shape[2]
    norm_sq = jnp.sum(wave * wave)
    energy = jnp.sum(wave * sigma) / norm_sq
    gap = onsite - energy
    first = (sigma - energy * wave) * gap / jnp.maximum(gap * gap, 1.0)
    correlation = jnp.sum(wave * first)
    second = first - correlation / norm_sq * wave
    length_sq = jnp.sum(second * second)
    correction = second * lax.rsqrt(length_sq / total + 1e-06)
    return (sigma, correction)
```

```python
import jax
import jax.numpy as jnp
from jax import lax
from jax.sharding import PartitionSpec as P


HIGH = lax.Precision.HIGH


def shifted(value, axis, by):
    length = lax.axis_size(axis)
    return lax.ppermute(value, axis, [(i, (i + by) % length) for i in range(length)])


def swapped(value, axis, bit):
    length = lax.axis_size(axis)
    return lax.ppermute(value, axis, [(i, i ^ bit) for i in range(length)])


def merged(state, merge):
    for axis in ("sector", "op"):
        length = lax.axis_size(axis)
        if length & (length - 1) == 0:
            bit = 1
            while bit < length:
                state = merge(state, swapped(state, axis, bit))
                bit *= 2
        else:
            total, other = state, state
            for _ in range(length - 1):
                other = shifted(other, axis, 1)
                total = merge(total, other)
            state = total
    return state


def gathered_pieces(own, inner):
    outer = lax.axis_size("op") // inner
    pieces = []
    here = own
    for step in range(outer):
        if step > 0:
            here = shifted(here, "op", inner)
        pieces.append((here, swapped(here, "op", 1)) if inner == 2 else (here,))
    return pieces


def on_device(wave, onsite, left_ops, right_ops, coupling):
    rows, width = wave.shape[1], wave.shape[2]
    ops = lax.axis_size("op")
    inner = 2 if ops % 2 == 0 else 1
    outer = ops // inner
    me = lax.axis_index("op")
    ring, side = me // inner, me % inner

    def assembled(steps):
        full = jnp.zeros((ops, rows, width), jnp.float32)
        for step, pieces in enumerate(steps):
            place = lax.rem(ring - step + outer, outer) * inner
            for index, piece in enumerate(pieces):
                at = place + (side if index == 0 else 1 - side)
                full = lax.dynamic_update_slice(full, piece[None], (at, 0, 0))
        return full.reshape(ops * rows, width)

    own0 = gathered_pieces(wave[0], inner)
    own1 = gathered_pieces(wave[1], inner)
    ahead0 = [tuple(jnp.unstack(shifted(jnp.stack(pieces), "sector", -1))) for pieces in own0]
    full0, full1, ahead = assembled(own0), assembled(own1), assembled(ahead0)

    weights = coupling.astype(jnp.float32)[:, :, None, None]
    x0 = weights[0] * jnp.einsum("kac,cb->kab", left_ops[0], full0, precision=HIGH)
    y1 = weights[1] * jnp.einsum("kca,cb->kab", left_ops[1], ahead, precision=HIGH)

    def chunk_of(value, place):
        return lax.dynamic_slice_in_dim(value, place * inner * rows, inner * rows, axis=value.ndim - 2)

    part_a = jnp.einsum("kab,kcb->ac", x0, right_ops[0], precision=HIGH) + jnp.einsum(
        "kab,kbc->ac", y1, right_ops[1], precision=HIGH
    )

    part_a, full1 = lax.optimization_barrier((part_a, full1))
    x1 = weights[1] * jnp.einsum("kac,cb->kab", left_ops[1], full1, precision=HIGH)
    y0 = weights[0] * jnp.einsum("kca,cb->kab", left_ops[0], full1, precision=HIGH)

    def chunk_a(place):
        return chunk_of(part_a, place)

    def chunk_b(place):
        leaving = jnp.einsum("kab,kcb->ac", chunk_of(x1, place), right_ops[1], precision=HIGH)
        arriving = shifted(leaving, "sector", 1)
        back = jnp.einsum("kab,kbc->ac", chunk_of(y0, place), right_ops[0], precision=HIGH)
        return back + arriving

    def reduced(chunk):
        acc = None
        for step in range(outer):
            part = chunk(lax.rem(ring - 1 - step + 2 * outer, outer))
            if inner == 2:
                mine = lax.dynamic_slice_in_dim(part, side * rows, rows, axis=0)
                other = lax.dynamic_slice_in_dim(part, (1 - side) * rows, rows, axis=0)
                part = mine + swapped(other, "op", 1)
            acc = part if acc is None else part + shifted(acc, "op", inner)
        return acc

    cross1 = reduced(chunk_a)
    cross0 = reduced(chunk_b)

    def by_column(value):
        return jnp.sum(value, axis=tuple(range(value.ndim - 1)))

    norm_local = by_column(wave * wave)
    energy_local = by_column(onsite * wave * wave) + 2.0 * by_column(wave[1] * cross1)
    norm_sq, energy_sum = jnp.unstack(jnp.sum(merged(jnp.stack([norm_local, energy_local]), jnp.add), axis=1))
    energy = energy_sum / norm_sq
    sigma = onsite * wave + jnp.stack([cross0, cross1])
    gap = onsite - energy
    first = (sigma - energy * wave) * gap / jnp.maximum(gap * gap, 1.0)

    def ratio(top, bottom):
        return jnp.where(bottom > 0.0, top / jnp.where(bottom > 0.0, bottom, 1.0), 0.0)

    corr_local = by_column(wave * first)
    rest = first - ratio(corr_local, norm_local) * wave
    rest_local = by_column(rest * rest)

    def merge(one, two):
        apart = ratio(one[1], one[0]) - ratio(two[1], two[0])
        return jnp.stack(
            [
                one[0] + two[0],
                one[1] + two[1],
                one[2] + two[2] + apart * apart * ratio(one[0] * two[0], one[0] + two[0]),
            ]
        )

    total = wave.shape[0] * rows * width * lax.axis_size("sector") * ops
    norms, corrs, rests = jnp.unstack(merged(jnp.stack([norm_local, corr_local, rest_local]), merge))
    along = jnp.sum(corrs) / jnp.sum(norms)
    apart = ratio(corrs, norms) - along
    length_sq = jnp.sum(rests + norms * apart * apart)
    second = first - along * wave
    correction = second * lax.rsqrt(length_sq / total + 1e-06)
    return (sigma, correction)


def solution(mesh):
    return jax.shard_map(
        on_device,
        mesh=mesh,
        in_specs=(
            P("sector", "op", None),
            P("sector", "op", None),
            P("sector", "op", None, None),
            P("sector", "op", None, None),
            P("sector", "op"),
        ),
        out_specs=(P("sector", "op", None), P("sector", "op", None)),
        check_vma=False,
    )
```
